256 devices in a mesh: rows: 256 (over x, z, y, core).
Axes of the slice: x: 4, y: 4, z: 8, core: 2. Of those that a mesh axis runs over, the one named last changes fastest.
Arguments:
- points_t: float32 [64, 262144], P(None, 'rows'), may hold values from -6 to 6
- pivots: int32 [2, 256], replicated, may hold values from 0 to 262143, as said below
Outputs:
- factor: bfloat16 [262144, 512], P('rows')
- residual_diag: float32 [262144], P('rows')
The draws below stay inside these ranges and needn't reach their ends.
Inputs may be any that keep to these rules, and one draw needn't show every extreme that they name: `pivots`: all 512 indices are different. In each block at most 3 indices fall in one device's points, rows k * 1024 to (k + 1) * 1024 - 1, and in each block some device holds exactly 3.
All inputs are finite; a program needn't handle non-finite values.
Results may differ from the reference program's by a relative error of at most 0.001.
Values sent between devices are 32-bit elements; how exact they have to be, the bound alone decides.
A program may use at most 64 MiB of HBM per device.

```python
import jax
import jax.numpy as jnp
from jax import lax

DIM = 64
PIV = 256
BLOCKS = 2
PTS_DEV = 1024
POINTS = 262144
CAP = 3


def draw_pivots(key, part):
    ndev = POINTS // PTS_DEV
    span = PTS_DEV // (3 * CAP)
    result = []
    for block in range(BLOCKS):
        kblock = jax.random.fold_in(key, 17 + block)
        kperm = jax.random.fold_in(kblock, 1)
        koff = jax.random.fold_in(kblock, 2)
        kshuf = jax.random.fold_in(kblock, 3)
        slots = jax.random.permutation(kperm, ndev * CAP).astype(jnp.int32)
        busiest = slots[0] // CAP
        full = busiest * CAP + jnp.arange(CAP, dtype=jnp.int32)
        owners = slots // CAP
        order_key = jnp.where(owners == busiest, ndev * CAP + jnp.arange(ndev * CAP, dtype=jnp.int32), jnp.arange(ndev * CAP, dtype=jnp.int32))
        order = jnp.argsort(order_key, stable=True)
        rest = slots[order][:PIV - CAP]
        chosen = jnp.concatenate([full, rest])
        owner = chosen // CAP
        sub = chosen % CAP
        offset = jax.random.randint(koff, (PIV,), 0, span).astype(jnp.int32)
        local = (block * CAP + sub) * span + offset
        index = owner * PTS_DEV + local
        shuffle = jax.random.permutation(kshuf, PIV)
        result.append(index[shuffle])
    return jnp.stack(result).astype(jnp.int32)


def steps_of(rng, extent, split, least, high):
    def one(axis_at, shards_of):
        draws = jax.random.uniform(jax.random.fold_in(jax.random.fold_in(rng, 6), axis_at), (shards_of,), jnp.float32, least / len(split), high / len(split))
        return jnp.repeat(jnp.exp(draws), extent[axis_at] // shards_of).reshape((-1,) + (1,) * (len(extent) - axis_at - 1))

    loudness = one(*split[0])
    for cut in split[1:]:
        loudness = loudness * one(*cut)
    return loudness


def scatter_about(rng, extent, spread, limit, pieces=(), held_as=jnp.bfloat16):
    entries = jax.random.normal(rng, extent, jnp.float32) * spread
    if len(pieces) > 0:
        entries = steps_of(rng, extent, pieces, -0.22, 0.18) * entries
    return jnp.clip(entries, min=-limit, max=limit).astype(held_as)


def setup_inputs(seed: int = 0) -> dict:
    keys = jax.random.split(jax.random.key(seed), 3)
    return {
        "points_t": scatter_about(keys[0], (DIM, POINTS), 1.0, 6.0, ((1, 256),), jnp.float32),
        "pivots": draw_pivots(jax.random.fold_in(keys[2], 71), 0),
    }


def kernel(left_t, right_t):
    cross = lax.dot_general(left_t.astype(jnp.float32), right_t.astype(jnp.float32), (((0,), (0,)), ((), ())), precision=lax.Precision.HIGHEST, preferred_element_type=jnp.float32)
    sq = jnp.sum(left_t * left_t, 0)[:, None] + jnp.sum(right_t * right_t, 0)[None, :] - 2.0 * cross
    return jnp.exp(-sq / (1.65 * DIM))

def reference(points_t, pivots):
    nblocks = POINTS // PTS_DEV
    point_blocks = points_t.reshape(DIM, nblocks, PTS_DEV).transpose(1, 0, 2)
    factor = jnp.zeros((POINTS, 0), jnp.float32)
    for block in range(BLOCKS):
        chosen = pivots[block]
        pivot_pts = points_t[:, chosen]
        pivot_rows = factor[chosen]
        pivot_block = kernel(pivot_pts, pivot_pts) - jnp.dot(pivot_rows.astype(jnp.float32), pivot_rows.T.astype(jnp.float32), precision=lax.Precision.HIGHEST, preferred_element_type=jnp.float32)
        lower = jnp.linalg.cholesky(pivot_block)
        inverse = jax.scipy.linalg.solve_triangular(lower, jnp.eye(PIV, dtype=jnp.float32), lower=True)
        factor_blocks = factor.reshape(nblocks, PTS_DEV, factor.shape[1])

        def one_block(pair):
            pts, rows = pair
            resid = kernel(pts, pivot_pts) - jnp.dot(rows.astype(jnp.float32), pivot_rows.T.astype(jnp.float32), precision=lax.Precision.HIGHEST, preferred_element_type=jnp.float32)
            return jnp.dot(resid.astype(jnp.float32), inverse.T.astype(jnp.float32), precision=lax.Precision.HIGHEST, preferred_element_type=jnp.float32)
        newcols = lax.map(one_block, (point_blocks, factor_blocks)).reshape(POINTS, PIV)
        factor = jnp.concatenate([factor, newcols], axis=1)
    residual_diag = 1.0 - jnp.sum(factor * factor, axis=1)
    return (factor.astype(jnp.bfloat16), residual_diag)
```

```python
import jax
import jax.numpy as jnp
from jax import lax
from jax.experimental import pallas as pl
from jax.experimental.pallas import tpu as pltpu
from jax.sharding import PartitionSpec as P

NX, NZ, NY, NC = 4, 8, 4, 2
CAP = 3
ROWS = 4
BIG = 1 << 24


def kernel(left_t, right_t):
    cross = lax.dot_general(
        left_t,
        right_t,
        (((0,), (0,)), ((), ())),
        precision=lax.Precision.HIGHEST,
        preferred_element_type=jnp.float32,
    )
    sq = jnp.sum(left_t * left_t, 0)[:, None] + jnp.sum(right_t * right_t, 0)[None, :] - 2.0 * cross
    return jnp.exp(-sq / (1.65 * left_t.shape[0]))


def exact_dot(left, right):
    return jnp.dot(left, right, precision=lax.Precision.HIGHEST, preferred_element_type=jnp.float32)


def exchange_kernel(piv_ref, pts_ref, out_ref, zs, zr, bs, br, as_, ar, cs, cr):
    me = lax.axis_index("rows")
    core = lax.rem(me, NC)
    y = lax.rem(me // NC, NY)
    z = lax.rem(me // (NC * NY), NZ)
    x = me // (NC * NY * NZ)
    a = x + core * (y - x)
    b = y + core * (x - y)

    def device(a_, b_, z_, core_):
        x_ = a_ + core * (b_ - a_)
        y_ = b_ + core * (a_ - b_)
        return ((x_ * NZ + z_) * NY + y_) * NC + core_

    def z_peer(k):
        return device(a, b, lax.rem(z + k, NZ), core)

    def b_peer(k):
        return device(a, lax.rem(b + k, 4), z, core)

    def a_peer(k):
        return device(lax.rem(a + k, 4), b, z, core)

    sibling = device(a, b, z, 1 - core)
    peers = (
        [z_peer(k) for k in range(1, NZ)]
        + [b_peer(k) for k in range(1, 4)]
        + [a_peer(k) for k in range(1, 4)]
        + [sibling]
    )
    barrier = pltpu.get_barrier_semaphore()
    for peer in peers:
        pl.semaphore_signal(barrier, inc=1, device_id=(peer,), device_id_type=pl.DeviceIdType.MESH)

    rows_here = pts_ref.shape[1]
    local = piv_ref[...] - me * rows_here
    key = jnp.where((local >= 0) & (local < rows_here), local, BIG)
    floor = jnp.full((2, 1), -1, jnp.int32)
    lanes = lax.broadcasted_iota(jnp.int32, (2, rows_here), 1)
    picks = []
    for _ in range(CAP):
        floor = jnp.min(jnp.where(key > floor, key, BIG), axis=1, keepdims=True)
        picks.append(jnp.where(lanes == floor, 1.0, 0.0).astype(jnp.float32))
    pick = jnp.concatenate(
        [p[0:1] for p in picks] + [jnp.zeros((1, rows_here), jnp.float32)]
        + [p[1:2] for p in picks] + [jnp.zeros((1, rows_here), jnp.float32)],
        axis=0,
    )
    slots = lax.dot_general(
        pick,
        pts_ref[...],
        (((1,), (1,)), ((), ())),
        precision=lax.Precision.HIGHEST,
        preferred_element_type=jnp.float32,
    )
    mine = core * 128 + a * 32 + b * 8 + z
    out_ref[pl.ds(mine, 1)] = jnp.concatenate([slots[0:4], slots[4:8]], axis=1).reshape(1, ROWS, 128)
    pl.semaphore_wait(barrier, len(peers))

    def send(start, count, send_sem, recv_sem, peer):
        part = out_ref.at[pl.ds(start, count)]
        copy = pltpu.make_async_remote_copy(
            src_ref=part,
            dst_ref=part,
            send_sem=send_sem,
            recv_sem=recv_sem,
            device_id=(peer,),
            device_id_type=pl.DeviceIdType.MESH,
        )
        copy.start()
        return copy

    def arrived(start, count, send_sem, recv_sem, peer):
        part = out_ref.at[pl.ds(start, count)]
        pltpu.make_async_remote_copy(
            src_ref=part,
            dst_ref=part,
            send_sem=send_sem,
            recv_sem=recv_sem,
            device_id=(peer,),
            device_id_type=pl.DeviceIdType.MESH,
        ).wait_recv()

    out = []
    for k in range(1, NZ):
        out.append(send(mine, 1, zs.at[k - 1], zr.at[k - 1], z_peer(k)))
    for k in range(1, NZ):
        arrived(core * 128 + a * 32 + b * 8 + lax.rem(z + NZ - k, NZ), 1, zs.at[k - 1], zr.at[k - 1], z_peer(k))
    for k in range(1, 4):
        out.append(send(core * 128 + a * 32 + b * 8, 8, bs.at[k - 1], br.at[k - 1], b_peer(k)))
    for k in range(1, 4):
        arrived(core * 128 + a * 32 + lax.rem(b + 4 - k, 4) * 8, 8, bs.at[k - 1], br.at[k - 1], b_peer(k))
    for k in range(1, 4):
        out.append(send(core * 128 + a * 32, 32, as_.at[k - 1], ar.at[k - 1], a_peer(k)))
    out.append(send(core * 128 + a * 32, 32, cs.at[0], cr.at[0], sibling))
    for k in range(1, 4):
        from_a = lax.rem(a + 4 - k, 4)
        arrived(core * 128 + from_a * 32, 32, as_.at[k - 1], ar.at[k - 1], a_peer(k))
        out.append(send(core * 128 + from_a * 32, 32, cs.at[k], cr.at[k], sibling))
    for k in range(4):
        from_a = lax.rem(b + 4 - k, 4)
        arrived((1 - core) * 128 + from_a * 32, 32, cs.at[k], cr.at[k], sibling)
    for copy in out:
        copy.wait_send()


def exchange(points_t, pivots):
    return pl.pallas_call(
        exchange_kernel,
        out_shape=jax.ShapeDtypeStruct((256, ROWS, 128), jnp.float32),
        in_specs=[pl.BlockSpec(memory_space=pltpu.VMEM)] * 2,
        out_specs=pl.BlockSpec(memory_space=pltpu.VMEM),
        scratch_shapes=[
            pltpu.SemaphoreType.DMA((7,)),
            pltpu.SemaphoreType.DMA((7,)),
            pltpu.SemaphoreType.DMA((3,)),
            pltpu.SemaphoreType.DMA((3,)),
            pltpu.SemaphoreType.DMA((3,)),
            pltpu.SemaphoreType.DMA((3,)),
            pltpu.SemaphoreType.DMA((4,)),
            pltpu.SemaphoreType.DMA((4,)),
        ],
        compiler_params=pltpu.CompilerParams(collective_id=0, has_side_effects=True),
        name="exchange",
    )(pivots, points_t)


def places(pivots, rows_here):
    owner = pivots // rows_here
    before = (owner[:, :, None] == owner[:, None, :]) & (pivots[:, None, :] < pivots[:, :, None])
    rank = jnp.sum(before.astype(jnp.int32), axis=2)
    core = owner % NC
    y = (owner // NC) % NY
    z = (owner // (NC * NY)) % NZ
    x = owner // (NC * NY * NZ)
    a = jnp.where(core == 0, x, y)
    b = jnp.where(core == 0, y, x)
    return (core * 128 + a * 32 + b * 8 + z) * ROWS + rank


def body(points_t, pivots):
    dim, rows_here = points_t.shape
    blocks, piv = pivots.shape
    place = places(pivots, rows_here)
    gathered = exchange(points_t, pivots).reshape(-1, 2, dim)
    pivot_pts = [jnp.take(gathered[:, block], place[block], axis=0).T for block in range(blocks)]
    eye_block = jnp.eye(piv, dtype=jnp.float32)
    factor = None
    for block in range(blocks):
        resid = kernel(points_t, pivot_pts[block])
        pivot_block = kernel(pivot_pts[block], pivot_pts[block])
        if factor is not None:
            pivot_rows = exact_dot(kernel(pivot_pts[1], pivot_pts[0]), inverse.T)
            resid = resid - exact_dot(factor, pivot_rows.T)
            pivot_block = pivot_block - exact_dot(pivot_rows, pivot_rows.T)
        lower = jnp.linalg.cholesky(pivot_block)
        inverse = jax.scipy.linalg.solve_triangular(lower, eye_block, lower=True)
        newcols = exact_dot(resid, inverse.T)
        factor = newcols if factor is None else jnp.concatenate([factor, newcols], axis=1)
    residual_diag = 1.0 - jnp.sum(factor * factor, axis=1)
    return (factor.astype(jnp.bfloat16), residual_diag)


def solution(mesh):
    return jax.shard_map(
        body,
        mesh=mesh,
        in_specs=(P(None, "rows"), P()),
        out_specs=(P("rows", None), P("rows")),
        check_vma=False,
    )
```

```python
import jax
import jax.numpy as jnp
from jax import lax
from jax.experimental import pallas as pl
from jax.experimental.pallas import tpu as pltpu
from jax.sharding import PartitionSpec as P

NX, NZ, NY, NC = 4, 8, 4, 2
CAP = 3
BIG = 1 << 24


def exchange_kernel(piv_ref, pts_ref, out_ref, zs, zr, bs, br, as_, ar, cs, cr):
    me = lax.axis_index("rows")
    core = lax.rem(me, NC)
    y = lax.rem(me // NC, NY)
    z = lax.rem(me // (NC * NY), NZ)
    x = me // (NC * NY * NZ)
    a = x + core * (y - x)
    b = y + core * (x - y)

    def device(a_, b_, z_, core_):
        x_ = a_ + core * (b_ - a_)
        y_ = b_ + core * (a_ - b_)
        return ((x_ * NZ + z_) * NY + y_) * NC + core_

    def z_peer(k):
        return device(a, b, lax.rem(z + k, NZ), core)

    def b_peer(k):
        return device(a, lax.rem(b + k, 4), z, core)

    def a_peer(k):
        return device(lax.rem(a + k, 4), b, z, core)

    sibling = device(a, b, z, 1 - core)
    peers = (
        [z_peer(k) for k in range(1, NZ)]
        + [b_peer(k) for k in range(1, 4)]
        + [a_peer(k) for k in range(1, 4)]
        + [sibling]
    )
    barrier = pltpu.get_barrier_semaphore()
    for peer in peers:
        pl.semaphore_signal(barrier, inc=1, device_id=(peer,), device_id_type=pl.DeviceIdType.MESH)

    rows_here = pts_ref.shape[1]
    local = piv_ref[...] - me * rows_here
    key = jnp.where((local >= 0) & (local < rows_here), local, BIG)
    floor = jnp.full((2, 1), -1, jnp.int32)
    lanes = lax.broadcasted_iota(jnp.int32, (2, rows_here), 1)
    picks = []
    for _ in range(CAP):
        floor = jnp.min(jnp.where(key > floor, key, BIG), axis=1, keepdims=True)
        picks.append(jnp.where(lanes == floor, 1.0, 0.0).astype(jnp.float32))
    pick = jnp.concatenate(
        [p[0:1] for p in picks] + [jnp.zeros((1, rows_here), jnp.float32)]
        + [p[1:2] for p in picks] + [jnp.zeros((1, rows_here), jnp.float32)],
        axis=0,
    )
    slots = lax.dot_general(
        pick,
        pts_ref[...],
        (((1,), (1,)), ((), ())),
        precision=lax.Precision.HIGHEST,
        preferred_element_type=jnp.float32,
    )
    mine = core * 128 + a * 32 + b * 8 + z
    both = jnp.concatenate([slots[0:4], slots[4:8]], axis=1)
    for s in range(CAP):
        out_ref[mine * CAP + s] = both[s : s + 1]
    pl.semaphore_wait(barrier, len(peers))

    def send(start, count, send_sem, recv_sem, peer):
        part = out_ref.at[pl.ds(start * CAP, count * CAP)]
        copy = pltpu.make_async_remote_copy(
            src_ref=part,
            dst_ref=part,
            send_sem=send_sem,
            recv_sem=recv_sem,
            device_id=(peer,),
            device_id_type=pl.DeviceIdType.MESH,
        )
        copy.start()
        return copy

    def arrived(start, count, send_sem, recv_sem, peer):
        part = out_ref.at[pl.ds(start * CAP, count * CAP)]
        pltpu.make_async_remote_copy(
            src_ref=part,
            dst_ref=part,
            send_sem=send_sem,
            recv_sem=recv_sem,
            device_id=(peer,),
            device_id_type=pl.DeviceIdType.MESH,
        ).wait_recv()

    out = []
    for k in range(1, NZ):
        out.append(send(mine, 1, zs.at[k - 1], zr.at[k - 1], z_peer(k)))
    for k in range(1, NZ):
        arrived(core * 128 + a * 32 + b * 8 + lax.rem(z + NZ - k, NZ), 1, zs.at[k - 1], zr.at[k - 1], z_peer(k))
    for k in range(1, 4):
        out.append(send(core * 128 + a * 32 + b * 8, 8, bs.at[k - 1], br.at[k - 1], b_peer(k)))
    for k in range(1, 4):
        arrived(core * 128 + a * 32 + lax.rem(b + 4 - k, 4) * 8, 8, bs.at[k - 1], br.at[k - 1], b_peer(k))
    for k in range(1, 4):
        out.append(send(core * 128 + a * 32, 32, as_.at[k - 1], ar.at[k - 1], a_peer(k)))
    out.append(send(core * 128 + a * 32, 32, cs.at[0], cr.at[0], sibling))
    for k in range(1, 4):
        from_a = lax.rem(a + 4 - k, 4)
        arrived(core * 128 + from_a * 32, 32, as_.at[k - 1], ar.at[k - 1], a_peer(k))
        out.append(send(core * 128 + from_a * 32, 32, cs.at[k], cr.at[k], sibling))
    for k in range(4):
        from_a = lax.rem(b + 4 - k, 4)
        arrived((1 - core) * 128 + from_a * 32, 32, cs.at[k], cr.at[k], sibling)
    for copy in out:
        copy.wait_send()


def exchange(points_t, pivots):
    return pl.pallas_call(
        exchange_kernel,
        out_shape=jax.ShapeDtypeStruct((256 * CAP, 1, 128), jnp.float32),
        in_specs=[pl.BlockSpec(memory_space=pltpu.VMEM)] * 2,
        out_specs=pl.BlockSpec(memory_space=pltpu.VMEM),
        scratch_shapes=[
            pltpu.SemaphoreType.DMA((7,)),
            pltpu.SemaphoreType.DMA((7,)),
            pltpu.SemaphoreType.DMA((3,)),
            pltpu.SemaphoreType.DMA((3,)),
            pltpu.SemaphoreType.DMA((3,)),
            pltpu.SemaphoreType.DMA((3,)),
            pltpu.SemaphoreType.DMA((4,)),
            pltpu.SemaphoreType.DMA((4,)),
        ],
        compiler_params=pltpu.CompilerParams(collective_id=0, has_side_effects=True),
        name="exchange",
    )(pivots, points_t)


def places(pivots, rows_here):
    owner = pivots // rows_here
    before = (owner[:, :, None] == owner[:, None, :]) & (pivots[:, None, :] < pivots[:, :, None])
    rank = jnp.sum(before.astype(jnp.int32), axis=2)
    core = owner % NC
    y = (owner // NC) % NY
    z = (owner // (NC * NY)) % NZ
    x = owner // (NC * NY * NZ)
    a = jnp.where(core == 0, x, y)
    b = jnp.where(core == 0, y, x)
    return (core * 128 + a * 32 + b * 8 + z) * CAP + rank


LANES = 128
HIGHEST = lax.Precision.HIGHEST


def nt(left, right):
    return lax.dot_general(left, right, (((1,), (1,)), ((), ())), precision=HIGHEST, preferred_element_type=jnp.float32)


def tn(left, right):
    return lax.dot_general(left, right, (((0,), (0,)), ((), ())), precision=HIGHEST, preferred_element_type=jnp.float32)


def spread(column):
    return jnp.broadcast_to(column, (8, LANES))


def factor_kernel(place_ref, g_ref, pts_ref, f_ref, r_ref, pv_ref, m_ref, s_ref, kx_ref, q_ref):
    dim, points = pts_ref.shape
    size = m_ref.shape[0]
    piv = size // 2
    wide = size // LANES
    scale = -1.0 / (1.65 * dim)

    for j in range(size):
        pv_ref[j : j + 1, :] = g_ref[place_ref[j]]
    pivots = jnp.concatenate([pv_ref[:piv, :dim], pv_ref[piv:, dim:]], axis=0)
    squared = pivots * pivots
    norm_row = nt(jnp.ones((8, dim), jnp.float32), squared)[0:1]
    norm_col = jnp.sum(squared, axis=1, keepdims=True)
    m_ref[...] = jnp.exp((norm_col + norm_row - 2.0 * nt(pivots, pivots)) * scale)

    pts = pts_ref[...].T
    norm_pts = jnp.sum(pts * pts, axis=1, keepdims=True)
    kx_ref[...] = jnp.exp((norm_pts + norm_row - 2.0 * nt(pts, pivots)) * scale)

    sub = lax.broadcasted_iota(jnp.int32, (8, LANES), 0)
    lane = lax.broadcasted_iota(jnp.int32, (8, LANES), 1)

    for blk in range(wide):
        start, end = blk * LANES, (blk + 1) * LANES
        for c0 in range(start, end, 8):
            off = c0 - start
            rows = [m_ref[c0 : c0 + 8, v * LANES : (v + 1) * LANES] for v in range(wide)]
            cols = [spread(rows[blk][:, off + k : off + k + 1]) for k in range(8)]
            own = (lane >= off) & (lane < off + 8)
            rows[blk] = jnp.where(own, jnp.where(lane - off == sub, 1.0, 0.0), rows[blk])
            kept = list(rows)
            diag = cols[0]
            for j in range(8):
                inv = spread((1.0 / cols[j])[j : j + 1])
                scaled = jnp.where(sub == j, 0.0, cols[j]) * inv
                if j:
                    diag = jnp.where(sub == j, cols[j], diag)
                    kept = [jnp.where(sub == j, r, s) for r, s in zip(rows, kept)]
                for k in range(j + 1, 8):
                    cols[k] = cols[k] - scaled * spread(cols[k][j : j + 1])
                rows = [r - scaled * spread(r[j : j + 1]) for r in rows]
            root = lax.rsqrt(diag)
            kept[blk] = jnp.where(lane < off + 8, kept[blk], 0.0)
            for v in range(wide):
                s_ref[c0 : c0 + 8, v * LANES : (v + 1) * LANES] = kept[v] * root
            inv = 1.0 / diag
            turned = [[spread((r * inv)[k : k + 1]) for k in range(8)] for r in rows]
            for r0 in range(c0 + 8, end, 8):
                old = [m_ref[r0 : r0 + 8, v * LANES : (v + 1) * LANES] for v in range(wide)]
                factors = [spread(old[blk][:, off + k : off + k + 1]) for k in range(8)]
                old[blk] = jnp.where(own, 0.0, old[blk])
                for v in range(wide):
                    new = old[v]
                    for k in range(8):
                        new = new - factors[k] * turned[v][k]
                    m_ref[r0 : r0 + 8, v * LANES : (v + 1) * LANES] = new
        if end < size:
            update = tn(s_ref[start:end, end:], s_ref[start:end, :])
            for v in range(wide):
                part = slice(v * LANES, (v + 1) * LANES)
                if v == blk:
                    m_ref[end:, part] = -update[:, part]
                else:
                    m_ref[end:, part] = m_ref[end:, part] - update[:, part]
        new = nt(kx_ref[:, :end], s_ref[start:end, :end])
        f_ref[:, start:end] = new.astype(jnp.bfloat16)
        q_ref[...] = new * new if blk == 0 else q_ref[...] + new * new
    r_ref[...] = 1.0 - nt(jnp.ones((8, LANES), jnp.float32), q_ref[...])[0:1]


def factor_call(place, gathered, points_t, size=512):
    dim, points = points_t.shape
    return pl.pallas_call(
        factor_kernel,
        out_shape=[
            jax.ShapeDtypeStruct((points, size), jnp.bfloat16),
            jax.ShapeDtypeStruct((1, points), jnp.float32),
        ],
        in_specs=[
            pl.BlockSpec(memory_space=pltpu.SMEM),
            pl.BlockSpec(memory_space=pltpu.VMEM),
            pl.BlockSpec(memory_space=pltpu.VMEM),
        ],
        out_specs=[pl.BlockSpec(memory_space=pltpu.VMEM)] * 2,
        scratch_shapes=[
            pltpu.VMEM((size, LANES), jnp.float32),
            pltpu.VMEM((size, size), jnp.float32),
            pltpu.VMEM((size, size), jnp.float32),
            pltpu.VMEM((points, size), jnp.float32),
            pltpu.VMEM((points, LANES), jnp.float32),
        ],
        compiler_params=pltpu.CompilerParams(vmem_limit_bytes=40 << 20),
        name="factor",
    )(place, gathered, points_t)


def body(points_t, pivots):
    place = places(pivots, points_t.shape[1]).reshape(-1)
    factor, resid = factor_call(place, exchange(points_t, pivots), points_t)
    return (factor, resid.reshape(-1))


def solution(mesh):
    return jax.shard_map(
        body,
        mesh=mesh,
        in_specs=(P(None, "rows"), P()),
        out_specs=(P("rows", None), P("rows")),
        check_vma=False,
    )
```

```python
import jax
import jax.numpy as jnp
from jax import lax
from jax.experimental import pallas as pl
from jax.experimental.pallas import tpu as pltpu
from jax.sharding import PartitionSpec as P

NX, NZ, NY, NC = 4, 8, 4, 2
CAP = 3
NEAR = 5
HALF = NX * NY * NZ * CAP
FAR_AT = NX * NY * NEAR * CAP
BIG = 1 << 24
MESH = pl.DeviceIdType.MESH


def exchange_kernel(piv_ref, pts_hbm, out_ref, place_ref, pts_ref, pts_sem, zs, zr, ps, pr, cs, cr):
    me = lax.axis_index("rows")
    core = lax.rem(me, NC)
    y = lax.rem(me // NC, NY)
    z = lax.rem(me // (NC * NY), NZ)
    x = me // (NC * NY * NZ)

    def device(x_, y_, z_, core_):
        return ((x_ * NZ + z_) * NY + y_) * NC + core_

    def z_peer(k):
        return device(x, y, lax.rem(z + k, NZ), core)

    flat = [(i, k) for i in range(NX) for k in range(NY) if i or k]

    def plane_peer(i, k):
        return device(lax.rem(x + i, NX), lax.rem(y + k, NY), z, core)

    sibling = device(x, y, z, 1 - core)
    peers = [z_peer(k) for k in range(1, NZ)] + [plane_peer(i, k) for i, k in flat] + [sibling]
    barrier = pltpu.get_barrier_semaphore()
    for peer in peers:
        pl.semaphore_signal(barrier, inc=1, device_id=(peer,), device_id_type=MESH)
    load = pltpu.make_async_copy(pts_hbm, pts_ref, pts_sem)
    load.start()

    rows_here = pts_ref.shape[1]
    pivots = piv_ref[...]
    local = pivots - me * rows_here
    key = jnp.where((local >= 0) & (local < rows_here), local, BIG)
    floor = jnp.full((2, 1), -1, jnp.int32)
    lanes = lax.broadcasted_iota(jnp.int32, (2, rows_here), 1)
    picks = []
    for _ in range(CAP):
        floor = jnp.min(jnp.where(key > floor, key, BIG), axis=1, keepdims=True)
        picks.append(jnp.where(lanes == floor, 1.0, 0.0).astype(jnp.float32))
    pad = jnp.zeros((1, rows_here), jnp.float32)
    pick = jnp.concatenate([p[0:1] for p in picks] + [pad] + [p[1:2] for p in picks] + [pad], axis=0)
    load.wait()
    slots = lax.dot_general(
        pick,
        pts_ref[...],
        (((1,), (1,)), ((), ())),
        precision=lax.Precision.HIGHEST,
        preferred_element_type=jnp.float32,
    )
    both = jnp.concatenate([slots[0:4], slots[4:8]], axis=1)

    def near_at(core_, plane):
        return core_ * HALF + plane * (NEAR * CAP)

    def far_at(core_, plane):
        return core_ * HALF + FAR_AT + plane * ((NZ - NEAR) * CAP)

    def chunk_at(core_, plane, step):
        zz = (step + 2) % NZ
        if zz < NEAR:
            return near_at(core_, plane) + zz * CAP
        return far_at(core_, plane) + (zz - NEAR) * CAP

    here = x * NY + y
    mine = chunk_at(core, here, 0)
    for s in range(CAP):
        out_ref[mine + s] = both[s : s + 1]
    pl.semaphore_wait(barrier, len(peers))

    def remote(src, dst, count, send_sem, recv_sem, peer):
        return pltpu.make_async_remote_copy(
            src_ref=out_ref.at[pl.ds(src, count)],
            dst_ref=out_ref.at[pl.ds(dst, count)],
            send_sem=send_sem,
            recv_sem=recv_sem,
            device_id=(peer,),
            device_id_type=MESH,
        )

    sent = []

    def send(*what):
        copy = remote(*what)
        copy.start()
        sent.append(copy)

    near_steps = [1, NZ - 1, 2, NZ - 2]
    far_steps = [k for k in range(1, NZ) if k not in near_steps]
    for k in far_steps + near_steps:
        send(mine, chunk_at(core, here, -k), CAP, zs.at[k - 1], zr.at[k - 1], z_peer(k))

    as_float = jnp.concatenate([pivots, jnp.zeros((6, pivots.shape[1]), jnp.int32)], axis=0).astype(jnp.float32)
    columns = jnp.transpose(as_float)
    ranks = []
    for block in range(2):
        other = columns[:, block : block + 1]
        row = as_float[block : block + 1]
        first = ((pivots[block : block + 1] // rows_here) * rows_here).astype(jnp.float32)
        before = (other < row) & (other >= first)
        ranks.append(jnp.sum(jnp.where(before, 1.0, 0.0), axis=0, keepdims=True))
    rank = jnp.concatenate(ranks, axis=0).astype(jnp.int32)
    owner = pivots // rows_here
    o_core = lax.rem(owner, NC)
    o_y = lax.rem(owner // NC, NY)
    o_z = lax.rem(owner // (NC * NY), NZ)
    o_x = owner // (NC * NY * NZ)
    o_plane = o_x * NY + o_y
    zz = lax.rem(o_z - z + (NZ + 2), NZ)
    place_ref[...] = (
        jnp.where(
            zz < NEAR,
            near_at(o_core, o_plane) + zz * CAP,
            far_at(o_core, o_plane) + (zz - NEAR) * CAP,
        )
        + rank
    )

    def z_arrived(k):
        remote(mine, chunk_at(core, here, -k), CAP, zs.at[k - 1], zr.at[k - 1], z_peer(k)).wait_recv()

    for group, steps, at, count in (
        (0, near_steps, near_at, NEAR * CAP),
        (1, far_steps, far_at, (NZ - NEAR) * CAP),
    ):
        for k in steps:
            z_arrived(k)
        for n, (i, k) in enumerate(flat):
            send(at(core, here), at(core, here), count, ps.at[group, n], pr.at[group, n], plane_peer(i, k))
    for group, at, count in ((0, near_at, NEAR * CAP), (1, far_at, (NZ - NEAR) * CAP)):
        for n, (i, k) in enumerate(flat):
            source = lax.rem(x + NX - i, NX) * NY + lax.rem(y + NY - k, NY)
            remote(at(core, source), at(core, source), count, ps.at[group, n], pr.at[group, n], plane_peer(i, k)).wait_recv()
        send(at(core, 0), at(core, 0), count * NX * NY, cs.at[group], cr.at[group], sibling)
    for group, at, count in ((0, near_at, NEAR * CAP), (1, far_at, (NZ - NEAR) * CAP)):
        remote(
            at(1 - core, 0), at(1 - core, 0), count * NX * NY, cs.at[group], cr.at[group], sibling
        ).wait_recv()
    for copy in sent:
        copy.wait_send()


def exchange(points_t, pivots):
    return pl.pallas_call(
        exchange_kernel,
        out_shape=[
            pltpu.VMEM((NC * HALF, 1, 128), jnp.float32),
            pltpu.VMEM(pivots.shape, jnp.int32),
        ],
        in_specs=[pl.BlockSpec(memory_space=pltpu.VMEM), pl.BlockSpec(memory_space=pl.ANY)],
        out_specs=[pl.BlockSpec(memory_space=pltpu.VMEM)] * 2,
        scratch_shapes=[
            pltpu.VMEM(points_t.shape, jnp.float32),
            pltpu.SemaphoreType.DMA(()),
            pltpu.SemaphoreType.DMA((NZ - 1,)),
            pltpu.SemaphoreType.DMA((NZ - 1,)),
            pltpu.SemaphoreType.DMA((2, NX * NY - 1)),
            pltpu.SemaphoreType.DMA((2, NX * NY - 1)),
            pltpu.SemaphoreType.DMA((2,)),
            pltpu.SemaphoreType.DMA((2,)),
        ],
        compiler_params=pltpu.CompilerParams(collective_id=0, has_side_effects=True),
        name="exchange",
    )(pivots, points_t)


LANES = 128
HIGHEST = lax.Precision.HIGHEST


def nt(left, right):
    return lax.dot_general(left, right, (((1,), (1,)), ((), ())), precision=HIGHEST, preferred_element_type=jnp.float32)


def tn(left, right):
    return lax.dot_general(left, right, (((0,), (0,)), ((), ())), precision=HIGHEST, preferred_element_type=jnp.float32)


def spread(column):
    return jnp.broadcast_to(column, (8, LANES))


def factor_kernel(place_ref, g_ref, pts_ref, f_ref, r_ref, pv_ref, m_ref, s_ref, kx_ref, q_ref):
    dim, points = pts_ref.shape
    size = m_ref.shape[0]
    piv = size // 2
    wide = size // LANES
    scale = -1.0 / (1.65 * dim)

    for j in range(size):
        pv_ref[j : j + 1, :] = g_ref[place_ref[j // piv, j % piv]]
    pivots = jnp.concatenate([pv_ref[:piv, :dim], pv_ref[piv:, dim:]], axis=0)
    squared = pivots * pivots
    norm_row = nt(jnp.ones((8, dim), jnp.float32), squared)[0:1]
    norm_col = jnp.sum(squared, axis=1, keepdims=True)
    m_ref[...] = jnp.exp((norm_col + norm_row - 2.0 * nt(pivots, pivots)) * scale)

    pts = pts_ref[...].T
    norm_pts = jnp.sum(pts * pts, axis=1, keepdims=True)
    kx_ref[...] = jnp.exp((norm_pts + norm_row - 2.0 * nt(pts, pivots)) * scale)

    sub = lax.broadcasted_iota(jnp.int32, (8, LANES), 0)
    lane = lax.broadcasted_iota(jnp.int32, (8, LANES), 1)

    for blk in range(wide):
        start, end = blk * LANES, (blk + 1) * LANES
        for c0 in range(start, end, 8):
            off = c0 - start
            rows = [m_ref[c0 : c0 + 8, v * LANES : (v + 1) * LANES] for v in range(wide)]
            cols = [spread(rows[blk][:, off + k : off + k + 1]) for k in range(8)]
            own = (lane >= off) & (lane < off + 8)
            rows[blk] = jnp.where(own, jnp.where(lane - off == sub, 1.0, 0.0), rows[blk])
            kept = list(rows)
            diag = cols[0]
            for j in range(8):
                inv = spread((1.0 / cols[j])[j : j + 1])
                scaled = jnp.where(sub == j, 0.0, cols[j]) * inv
                if j:
                    diag = jnp.where(sub == j, cols[j], diag)
                    kept = [jnp.where(sub == j, r, s) for r, s in zip(rows, kept)]
                for k in range(j + 1, 8):
                    cols[k] = cols[k] - scaled * spread(cols[k][j : j + 1])
                rows = [r - scaled * spread(r[j : j + 1]) for r in rows]
            root = lax.rsqrt(diag)
            kept[blk] = jnp.where(lane < off + 8, kept[blk], 0.0)
            for v in range(wide):
                s_ref[c0 : c0 + 8, v * LANES : (v + 1) * LANES] = kept[v] * root
            inv = 1.0 / diag
            turned = [[spread((r * inv)[k : k + 1]) for k in range(8)] for r in rows]
            for r0 in range(c0 + 8, end, 8):
                old = [m_ref[r0 : r0 + 8, v * LANES : (v + 1) * LANES] for v in range(wide)]
                factors = [spread(old[blk][:, off + k : off + k + 1]) for k in range(8)]
                old[blk] = jnp.where(own, 0.0, old[blk])
                for v in range(wide):
                    new = old[v]
                    for k in range(8):
                        new = new - factors[k] * turned[v][k]
                    m_ref[r0 : r0 + 8, v * LANES : (v + 1) * LANES] = new
        if end < size:
            update = tn(s_ref[start:end, end:], s_ref[start:end, :])
            for v in range(wide):
                part = slice(v * LANES, (v + 1) * LANES)
                if v == blk:
                    m_ref[end:, part] = -update[:, part]
                else:
                    m_ref[end:, part] = m_ref[end:, part] - update[:, part]
        new = nt(kx_ref[:, :end], s_ref[start:end, :end])
        f_ref[:, start:end] = new.astype(jnp.bfloat16)
        q_ref[...] = new * new if blk == 0 else q_ref[...] + new * new
    r_ref[...] = 1.0 - nt(jnp.ones((8, LANES), jnp.float32), q_ref[...])[0:1]


def factor_call(place, gathered, points_t, size=512):
    dim, points = points_t.shape
    return pl.pallas_call(
        factor_kernel,
        out_shape=[
            jax.ShapeDtypeStruct((points, size), jnp.bfloat16),
            jax.ShapeDtypeStruct((1, points), jnp.float32),
        ],
        in_specs=[
            pl.BlockSpec(memory_space=pltpu.SMEM),
            pl.BlockSpec(memory_space=pltpu.VMEM),
            pl.BlockSpec(memory_space=pltpu.VMEM),
        ],
        out_specs=[pl.BlockSpec(memory_space=pltpu.VMEM)] * 2,
        scratch_shapes=[
            pltpu.VMEM((size, LANES), jnp.float32),
            pltpu.VMEM((size, size), jnp.float32),
            pltpu.VMEM((size, size), jnp.float32),
            pltpu.VMEM((points, size), jnp.float32),
            pltpu.VMEM((points, LANES), jnp.float32),
        ],
        compiler_params=pltpu.CompilerParams(vmem_limit_bytes=40 << 20),
        name="factor",
    )(place, gathered, points_t)


def body(points_t, pivots):
    gathered, place = exchange(points_t, pivots)
    factor, resid = factor_call(place, gathered, points_t)
    return (factor, resid.reshape(-1))


def solution(mesh):
    return jax.shard_map(
        body,
        mesh=mesh,
        in_specs=(P(None, "rows"), P()),
        out_specs=(P("rows", None), P("rows")),
        check_vma=False,
    )
```

```python
import jax
import jax.numpy as jnp
from jax import lax
from jax.experimental import pallas as pl
from jax.experimental.pallas import tpu as pltpu
from jax.sharding import PartitionSpec as P

NX, NZ, NY, NC = 4, 8, 4, 2
CAP = 3
NEAR = 5
HALF = NX * NY * NZ * CAP
FAR_AT = NX * NY * NEAR * CAP
BIG = 1 << 24
MESH = pl.DeviceIdType.MESH


def exchange_kernel(piv_ref, pts_hbm, out_ref, place_ref, pts_ref, pts_sem, zs, zr, ps, pr, cs, cr):
    me = lax.axis_index("rows")
    core = lax.rem(me, NC)
    y = lax.rem(me // NC, NY)
    z = lax.rem(me // (NC * NY), NZ)
    x = me // (NC * NY * NZ)

    def device(x_, y_, z_, core_):
        return ((x_ * NZ + z_) * NY + y_) * NC + core_

    def z_peer(k):
        return device(x, y, lax.rem(z + k, NZ), core)

    flat = [(i, k) for i in range(NX) for k in range(NY) if i or k]

    def plane_peer(i, k):
        return device(lax.rem(x + i, NX), lax.rem(y + k, NY), z, core)

    sibling = device(x, y, z, 1 - core)
    peers = [z_peer(k) for k in range(1, NZ)] + [plane_peer(i, k) for i, k in flat] + [sibling]
    barrier = pltpu.get_barrier_semaphore()
    for peer in peers:
        pl.semaphore_signal(barrier, inc=1, device_id=(peer,), device_id_type=MESH)
    load = pltpu.make_async_copy(pts_hbm, pts_ref, pts_sem)
    load.start()

    rows_here = pts_ref.shape[1]
    pivots = piv_ref[...]
    local = pivots - me * rows_here
    key = jnp.where((local >= 0) & (local < rows_here), local, BIG)
    floor = jnp.full((2, 1), -1, jnp.int32)
    lanes = lax.broadcasted_iota(jnp.int32, (2, rows_here), 1)
    picks = []
    for _ in range(CAP):
        floor = jnp.min(jnp.where(key > floor, key, BIG), axis=1, keepdims=True)
        picks.append(jnp.where(lanes == floor, 1.0, 0.0).astype(jnp.float32))
    pad = jnp.zeros((1, rows_here), jnp.float32)
    pick = jnp.concatenate([p[0:1] for p in picks] + [pad] + [p[1:2] for p in picks] + [pad], axis=0)
    load.wait()
    slots = lax.dot_general(
        pick,
        pts_ref[...],
        (((1,), (1,)), ((), ())),
        precision=lax.Precision.HIGHEST,
        preferred_element_type=jnp.float32,
    )
    both = jnp.concatenate([slots[0:4], slots[4:8]], axis=1)

    def near_at(core_, plane):
        return core_ * HALF + plane * (NEAR * CAP)

    def far_at(core_, plane):
        return core_ * HALF + FAR_AT + plane * ((NZ - NEAR) * CAP)

    def chunk_at(core_, plane, step):
        zz = (step + 2) % NZ
        if zz < NEAR:
            return near_at(core_, plane) + zz * CAP
        return far_at(core_, plane) + (zz - NEAR) * CAP

    here = x * NY + y
    mine = chunk_at(core, here, 0)
    for s in range(CAP):
        out_ref[mine + s] = both[s : s + 1]
    pl.semaphore_wait(barrier, len(peers))

    def remote(src, dst, count, send_sem, recv_sem, peer):
        return pltpu.make_async_remote_copy(
            src_ref=out_ref.at[pl.ds(src, count)],
            dst_ref=out_ref.at[pl.ds(dst, count)],
            send_sem=send_sem,
            recv_sem=recv_sem,
            device_id=(peer,),
            device_id_type=MESH,
        )

    sent = []

    def send(*what):
        copy = remote(*what)
        copy.start()
        sent.append(copy)

    near_steps = [1, NZ - 1, 2, NZ - 2]
    far_steps = [k for k in range(1, NZ) if k not in near_steps]
    for k in far_steps + near_steps:
        send(mine, chunk_at(core, here, -k), CAP, zs.at[k - 1], zr.at[k - 1], z_peer(k))

    as_float = jnp.concatenate([pivots, jnp.zeros((6, pivots.shape[1]), jnp.int32)], axis=0).astype(jnp.float32)
    columns = jnp.transpose(as_float)
    ranks = []
    for block in range(2):
        other = columns[:, block : block + 1]
        row = as_float[block : block + 1]
        first = ((pivots[block : block + 1] // rows_here) * rows_here).astype(jnp.float32)
        before = (other < row) & (other >= first)
        ranks.append(jnp.sum(jnp.where(before, 1.0, 0.0), axis=0, keepdims=True))
    rank = jnp.concatenate(ranks, axis=0).astype(jnp.int32)
    owner = pivots // rows_here
    o_core = lax.rem(owner, NC)
    o_y = lax.rem(owner // NC, NY)
    o_z = lax.rem(owner // (NC * NY), NZ)
    o_x = owner // (NC * NY * NZ)
    o_plane = o_x * NY + o_y
    zz = lax.rem(o_z - z + (NZ + 2), NZ)
    place_ref[...] = (
        jnp.where(
            zz < NEAR,
            near_at(o_core, o_plane) + zz * CAP,
            far_at(o_core, o_plane) + (zz - NEAR) * CAP,
        )
        + rank
    )

    def z_arrived(k):
        remote(mine, chunk_at(core, here, -k), CAP, zs.at[k - 1], zr.at[k - 1], z_peer(k)).wait_recv()

    for group, steps, at, count in (
        (0, near_steps, near_at, NEAR * CAP),
        (1, far_steps, far_at, (NZ - NEAR) * CAP),
    ):
        for k in steps:
            z_arrived(k)
        for n, (i, k) in enumerate(flat):
            send(at(core, here), at(core, here), count, ps.at[group, n], pr.at[group, n], plane_peer(i, k))
    for group, at, count in ((0, near_at, NEAR * CAP), (1, far_at, (NZ - NEAR) * CAP)):
        for n, (i, k) in enumerate(flat):
            source = lax.rem(x + NX - i, NX) * NY + lax.rem(y + NY - k, NY)
            remote(at(core, source), at(core, source), count, ps.at[group, n], pr.at[group, n], plane_peer(i, k)).wait_recv()
        send(at(core, 0), at(core, 0), count * NX * NY, cs.at[group], cr.at[group], sibling)
    for group, at, count in ((0, near_at, NEAR * CAP), (1, far_at, (NZ - NEAR) * CAP)):
        remote(
            at(1 - core, 0), at(1 - core, 0), count * NX * NY, cs.at[group], cr.at[group], sibling
        ).wait_recv()
    for copy in sent:
        copy.wait_send()


def exchange(points_t, pivots):
    return pl.pallas_call(
        exchange_kernel,
        out_shape=[
            pltpu.VMEM((NC * HALF, 1, 128), jnp.float32),
            pltpu.VMEM(pivots.shape, jnp.int32),
        ],
        in_specs=[pl.BlockSpec(memory_space=pltpu.VMEM), pl.BlockSpec(memory_space=pl.ANY)],
        out_specs=[pl.BlockSpec(memory_space=pltpu.VMEM)] * 2,
        scratch_shapes=[
            pltpu.VMEM(points_t.shape, jnp.float32),
            pltpu.SemaphoreType.DMA(()),
            pltpu.SemaphoreType.DMA((NZ - 1,)),
            pltpu.SemaphoreType.DMA((NZ - 1,)),
            pltpu.SemaphoreType.DMA((2, NX * NY - 1)),
            pltpu.SemaphoreType.DMA((2, NX * NY - 1)),
            pltpu.SemaphoreType.DMA((2,)),
            pltpu.SemaphoreType.DMA((2,)),
        ],
        compiler_params=pltpu.CompilerParams(collective_id=0, has_side_effects=True),
        name="exchange",
    )(pivots, points_t)


LANES = 128
HIGHEST = lax.Precision.HIGHEST
CHUNK = 256


def nt(left, right, precision=HIGHEST):
    return lax.dot_general(left, right, (((1,), (1,)), ((), ())), precision=precision, preferred_element_type=jnp.float32)


def nn(left, right):
    return lax.dot_general(left, right, (((1,), (0,)), ((), ())), precision=HIGHEST, preferred_element_type=jnp.float32)


def spread(column):
    return jnp.broadcast_to(column, (8, LANES))


def halves(value):
    high = value.astype(jnp.bfloat16)
    return high, (value - high.astype(jnp.float32)).astype(jnp.bfloat16)


def factor_kernel(place_ref, g_ref, pts_ref, f_ref, r_ref, pv_ref, m_ref, s_ref, l_ref, w_ref, kh_ref, kl_ref, g_last_ref, q_ref):
    dim, points = pts_ref.shape
    size = m_ref.shape[0]
    piv = size // 2
    wide = size // LANES
    scale = -1.0 / (1.65 * dim)

    for j in range(size):
        pv_ref[j : j + 1, :] = g_ref[place_ref[j // piv, j % piv]]
    pivots = jnp.concatenate([pv_ref[:piv, :dim], pv_ref[piv:, dim:]], axis=0)
    squared = pivots * pivots
    norm_row = nt(jnp.ones((8, dim), jnp.float32), squared)[0:1]
    norm_col = jnp.sum(squared, axis=1, keepdims=True)
    m_ref[...] = jnp.exp((norm_col + norm_row - 2.0 * nt(pivots, pivots)) * scale)

    pts = pts_ref[...].T
    norm_pts = jnp.sum(pts * pts, axis=1, keepdims=True)
    kx = jnp.exp((norm_pts + norm_row - 2.0 * nt(pts, pivots)) * scale)
    g_last_ref[...] = kx[:, size - LANES :]
    kh, kl = halves(kx)
    kh_ref[...] = kh
    kl_ref[...] = kl

    sub = lax.broadcasted_iota(jnp.int32, (8, LANES), 0)
    lane = lax.broadcasted_iota(jnp.int32, (8, LANES), 1)

    def lanes(v):
        return slice(v * LANES, (v + 1) * LANES)

    trail = []
    bulk = []

    def pump(queue, count):
        for _ in range(min(count, len(queue))):
            queue.pop(0)()

    def diagonal(blk):
        start = blk * LANES
        part = [m_ref[start + 8 * g : start + 8 * g + 8, lanes(blk)] for g in range(LANES // 8)]

        def update(g, off, own, turned):
            factors = [spread(part[g][:, off + k : off + k + 1]) for k in range(8)]
            new = jnp.where(own, 0.0, part[g])
            for k in range(8):
                new = new - factors[k] * turned[k]
            part[g] = new

        for g in range(len(part)):
            off = 8 * g
            rows = part[g]
            cols = [spread(rows[:, off + k : off + k + 1]) for k in range(8)]
            own = (lane >= off) & (lane < off + 8)
            rows = jnp.where(own, jnp.where(lane - off == sub, 1.0, 0.0), rows)
            kept = rows
            diag = cols[0]
            share = -(-len(trail) // 7)
            bulk_share = -(-len(bulk) // ((len(part) - g) * 4))
            for j in range(8):
                inv = spread((1.0 / cols[j])[j : j + 1])
                scaled = jnp.where(sub == j, 0.0, cols[j]) * inv
                if j:
                    diag = jnp.where(sub == j, cols[j], diag)
                    kept = jnp.where(sub == j, rows, kept)
                for k in range(j + 1, 8):
                    cols[k] = cols[k] - scaled * spread(cols[k][j : j + 1])
                rows = rows - scaled * spread(rows[j : j + 1])
                pump(trail, share)
                if j % 2:
                    pump(bulk, bulk_share)
            pump(trail, len(trail))
            rows = rows * (1.0 / diag)
            turned = [spread(rows[k : k + 1]) for k in range(8)]
            kept = jnp.where(lane < off + 8, kept, 0.0) * lax.rsqrt(diag)
            s_ref[start + off : start + off + 8, lanes(blk)] = kept
            if g + 1 < len(part):
                update(g + 1, off, own, turned)
            for h in range(g + 2, len(part)):
                trail.append(lambda h=h, off=off, own=own, turned=turned: update(h, off, own, turned))
        pump(bulk, len(bulk))

    def block(ref, r, c):
        return ref[r * LANES : (r + 1) * LANES, lanes(c)]

    def put_upper(blk, c):
        s_ref[blk * LANES : (blk + 1) * LANES, lanes(c)] = nn(block(s_ref, blk, blk), block(m_ref, blk, c))

    def put_lower(blk, r):
        l_ref[r * LANES : (r + 1) * LANES, :] = nt(block(m_ref, r, blk), block(s_ref, blk, blk))

    def put_outer(blk, r, c):
        change = nn(l_ref[r * LANES : (r + 1) * LANES, :], block(s_ref, blk, c))
        old = 0.0 if c == blk else block(m_ref, r, c)
        m_ref[r * LANES : (r + 1) * LANES, lanes(c)] = old - change

    def finish(new, part, c):
        f_ref[part, lanes(c)] = new.astype(jnp.bfloat16)
        q_ref[part, :] = new * new if c == 0 else q_ref[part, :] + new * new

    def product(left_high, left_low, weights):
        both = nt(left_high, weights, None) + nt(left_low, weights, None)
        return both[:, :LANES] + both[:, LANES:]

    def put_factor(blk, r0):
        part = slice(r0, r0 + CHUNK)
        width = (blk + 1) * LANES
        weights = w_ref[blk % 2, :, :width]
        finish(product(kh_ref[part, :width], kl_ref[part, :width], weights), part, blk)

    def put_weights(blk, value):
        high, low = halves(value)
        w_ref[blk % 2, :LANES, : value.shape[1]] = high
        w_ref[blk % 2, LANES:, : value.shape[1]] = low

    last = wide - 1

    def put_rest(r0):
        part = slice(r0, r0 + CHUNK)
        width = last * LANES
        new = product(kh_ref[part, :width], kl_ref[part, :width], w_ref[last % 2, :, :width])
        high, low = halves(g_last_ref[part, :] + new)
        kh_ref[part, lanes(last)] = high
        kl_ref[part, lanes(last)] = low

    for blk in range(wide):
        diagonal(blk)
        if blk == last:
            break
        put_upper(blk, blk + 1)
        put_lower(blk, blk + 1)
        put_outer(blk, blk + 1, blk + 1)

        def later(blk=blk):
            others = [c for c in range(wide) if c not in (blk, blk + 1)]
            for c in others:
                bulk.append(lambda c=c: put_upper(blk, c))
            for c in others + [blk]:
                bulk.append(lambda c=c: put_outer(blk, blk + 1, c))
            for r in range(blk + 2, wide):
                bulk.append(lambda r=r: put_lower(blk, r))
                for c in range(wide):
                    bulk.append(lambda r=r, c=c: put_outer(blk, r, c))
            if blk + 1 == last:
                bulk.append(lambda: put_weights(last, m_ref[last * LANES :, : last * LANES]))
                for r0 in range(0, points, CHUNK):
                    bulk.append(lambda r0=r0: put_rest(r0))
            bulk.append(lambda: put_weights(blk, s_ref[blk * LANES : (blk + 1) * LANES, : (blk + 1) * LANES]))
            for r0 in range(0, points, CHUNK):
                bulk.append(lambda r0=r0: put_factor(blk, r0))

        later()
    tail = jnp.concatenate(halves(block(s_ref, last, last)), axis=0)
    for r0 in range(0, points, CHUNK):
        part = slice(r0, r0 + CHUNK)
        finish(product(kh_ref[part, lanes(last)], kl_ref[part, lanes(last)], tail), part, last)
    r_ref[...] = 1.0 - nt(jnp.ones((8, LANES), jnp.float32), q_ref[...])[0:1]


def factor_call(place, gathered, points_t, size=512):
    dim, points = points_t.shape
    return pl.pallas_call(
        factor_kernel,
        out_shape=[
            jax.ShapeDtypeStruct((points, size), jnp.bfloat16),
            jax.ShapeDtypeStruct((1, points), jnp.float32),
        ],
        in_specs=[
            pl.BlockSpec(memory_space=pltpu.SMEM),
            pl.BlockSpec(memory_space=pltpu.VMEM),
            pl.BlockSpec(memory_space=pltpu.VMEM),
        ],
        out_specs=[pl.BlockSpec(memory_space=pltpu.VMEM)] * 2,
        scratch_shapes=[
            pltpu.VMEM((size, LANES), jnp.float32),
            pltpu.VMEM((size, size), jnp.float32),
            pltpu.VMEM((size, size), jnp.float32),
            pltpu.VMEM((size, LANES), jnp.float32),
            pltpu.VMEM((2, 2 * LANES, size), jnp.bfloat16),
            pltpu.VMEM((points, size), jnp.bfloat16),
            pltpu.VMEM((points, size), jnp.bfloat16),
            pltpu.VMEM((points, LANES), jnp.float32),
            pltpu.VMEM((points, LANES), jnp.float32),
        ],
        compiler_params=pltpu.CompilerParams(vmem_limit_bytes=40 << 20),
        name="factor",
    )(place, gathered, points_t)


def body(points_t, pivots):
    gathered, place = exchange(points_t, pivots)
    factor, resid = factor_call(place, gathered, points_t)
    return (factor, resid.reshape(-1))


def solution(mesh):
    return jax.shard_map(
        body,
        mesh=mesh,
        in_specs=(P(None, "rows"), P()),
        out_specs=(P("rows", None), P("rows")),
        check_vma=False,
    )
```

```python
import jax
import jax.numpy as jnp
from jax import lax
from jax.experimental import pallas as pl
from jax.experimental.pallas import tpu as pltpu
from jax.sharding import PartitionSpec as P

NX, NZ, NY, NC = 4, 8, 4, 2
CAP = 3
NEAR = 5
HALF = NX * NY * NZ * CAP
FAR_AT = NX * NY * NEAR * CAP
BIG = 1 << 24
MESH = pl.DeviceIdType.MESH


def exchange_kernel(piv_ref, pts_hbm, out_ref, place_ref, pts_ref, pts_sem, zs, zr, ps, pr, cs, cr):
    me = lax.axis_index("rows")
    core = lax.rem(me, NC)
    y = lax.rem(me // NC, NY)
    z = lax.rem(me // (NC * NY), NZ)
    x = me // (NC * NY * NZ)

    def device(x_, y_, z_, core_):
        return ((x_ * NZ + z_) * NY + y_) * NC + core_

    def z_peer(k):
        return device(x, y, lax.rem(z + k, NZ), core)

    flat = [(i, k) for i in range(NX) for k in range(NY) if i or k]

    def plane_peer(i, k):
        return device(lax.rem(x + i, NX), lax.rem(y + k, NY), z, core)

    sibling = device(x, y, z, 1 - core)
    peers = [z_peer(k) for k in range(1, NZ)] + [plane_peer(i, k) for i, k in flat] + [sibling]
    barrier = pltpu.get_barrier_semaphore()
    for peer in peers:
        pl.semaphore_signal(barrier, inc=1, device_id=(peer,), device_id_type=MESH)
    load = pltpu.make_async_copy(pts_hbm, pts_ref, pts_sem)
    load.start()

    rows_here = pts_ref.shape[1]
    pivots = piv_ref[...]
    local = pivots - me * rows_here
    key = jnp.where((local >= 0) & (local < rows_here), local, BIG)
    floor = jnp.full((2, 1), -1, jnp.int32)
    lanes = lax.broadcasted_iota(jnp.int32, (2, rows_here), 1)
    picks = []
    for _ in range(CAP):
        floor = jnp.min(jnp.where(key > floor, key, BIG), axis=1, keepdims=True)
        picks.append(jnp.where(lanes == floor, 1.0, 0.0).astype(jnp.float32))
    pad = jnp.zeros((1, rows_here), jnp.float32)
    pick = jnp.concatenate([p[0:1] for p in picks] + [pad] + [p[1:2] for p in picks] + [pad], axis=0)
    load.wait()
    slots = lax.dot_general(
        pick,
        pts_ref[...],
        (((1,), (1,)), ((), ())),
        precision=lax.Precision.HIGHEST,
        preferred_element_type=jnp.float32,
    )
    both = jnp.concatenate([slots[0:4], slots[4:8]], axis=1)

    def near_at(core_, plane):
        return core_ * HALF + plane * (NEAR * CAP)

    def far_at(core_, plane):
        return core_ * HALF + FAR_AT + plane * ((NZ - NEAR) * CAP)

    def chunk_at(core_, plane, step):
        zz = (step + 2) % NZ
        if zz < NEAR:
            return near_at(core_, plane) + zz * CAP
        return far_at(core_, plane) + (zz - NEAR) * CAP

    here = x * NY + y
    mine = chunk_at(core, here, 0)
    for s in range(CAP):
        out_ref[mine + s] = both[s : s + 1]
    pl.semaphore_wait(barrier, len(peers))

    def remote(src, dst, count, send_sem, recv_sem, peer):
        return pltpu.make_async_remote_copy(
            src_ref=out_ref.at[pl.ds(src, count)],
            dst_ref=out_ref.at[pl.ds(dst, count)],
            send_sem=send_sem,
            recv_sem=recv_sem,
            device_id=(peer,),
            device_id_type=MESH,
        )

    sent = []

    def send(*what):
        copy = remote(*what)
        copy.start()
        sent.append(copy)

    near_steps = [1, NZ - 1, 2, NZ - 2]
    far_steps = [k for k in range(1, NZ) if k not in near_steps]
    for k in far_steps + near_steps:
        send(mine, chunk_at(core, here, -k), CAP, zs.at[k - 1], zr.at[k - 1], z_peer(k))

    as_float = jnp.concatenate([pivots, jnp.zeros((6, pivots.shape[1]), jnp.int32)], axis=0).astype(jnp.float32)
    columns = jnp.transpose(as_float)
    ranks = []
    for block in range(2):
        other = columns[:, block : block + 1]
        row = as_float[block : block + 1]
        first = ((pivots[block : block + 1] // rows_here) * rows_here).astype(jnp.float32)
        before = (other < row) & (other >= first)
        ranks.append(jnp.sum(jnp.where(before, 1.0, 0.0), axis=0, keepdims=True))
    rank = jnp.concatenate(ranks, axis=0).astype(jnp.int32)
    owner = pivots // rows_here
    o_core = lax.rem(owner, NC)
    o_y = lax.rem(owner // NC, NY)
    o_z = lax.rem(owner // (NC * NY), NZ)
    o_x = owner // (NC * NY * NZ)
    o_plane = o_x * NY + o_y
    zz = lax.rem(o_z - z + (NZ + 2), NZ)
    place_ref[...] = (
        jnp.where(
            zz < NEAR,
            near_at(o_core, o_plane) + zz * CAP,
            far_at(o_core, o_plane) + (zz - NEAR) * CAP,
        )
        + rank
    )

    def z_arrived(k):
        remote(mine, chunk_at(core, here, -k), CAP, zs.at[k - 1], zr.at[k - 1], z_peer(k)).wait_recv()

    for group, steps, at, count in (
        (0, near_steps, near_at, NEAR * CAP),
        (1, far_steps, far_at, (NZ - NEAR) * CAP),
    ):
        for k in steps:
            z_arrived(k)
        for n, (i, k) in enumerate(flat):
            send(at(core, here), at(core, here), count, ps.at[group, n], pr.at[group, n], plane_peer(i, k))
    for group, at, count in ((0, near_at, NEAR * CAP), (1, far_at, (NZ - NEAR) * CAP)):
        for n, (i, k) in enumerate(flat):
            source = lax.rem(x + NX - i, NX) * NY + lax.rem(y + NY - k, NY)
            remote(at(core, source), at(core, source), count, ps.at[group, n], pr.at[group, n], plane_peer(i, k)).wait_recv()
        send(at(core, 0), at(core, 0), count * NX * NY, cs.at[group], cr.at[group], sibling)
    for group, at, count in ((0, near_at, NEAR * CAP), (1, far_at, (NZ - NEAR) * CAP)):
        remote(
            at(1 - core, 0), at(1 - core, 0), count * NX * NY, cs.at[group], cr.at[group], sibling
        ).wait_recv()
    for copy in sent:
        copy.wait_send()


def exchange(points_t, pivots):
    return pl.pallas_call(
        exchange_kernel,
        out_shape=[
            pltpu.VMEM((NC * HALF, 1, 128), jnp.float32),
            pltpu.VMEM(pivots.shape, jnp.int32),
        ],
        in_specs=[pl.BlockSpec(memory_space=pltpu.VMEM), pl.BlockSpec(memory_space=pl.ANY)],
        out_specs=[pl.BlockSpec(memory_space=pltpu.VMEM)] * 2,
        scratch_shapes=[
            pltpu.VMEM(points_t.shape, jnp.float32),
            pltpu.SemaphoreType.DMA(()),
            pltpu.SemaphoreType.DMA((NZ - 1,)),
            pltpu.SemaphoreType.DMA((NZ - 1,)),
            pltpu.SemaphoreType.DMA((2, NX * NY - 1)),
            pltpu.SemaphoreType.DMA((2, NX * NY - 1)),
            pltpu.SemaphoreType.DMA((2,)),
            pltpu.SemaphoreType.DMA((2,)),
        ],
        compiler_params=pltpu.CompilerParams(collective_id=0, has_side_effects=True),
        name="exchange",
    )(pivots, points_t)


LANES = 128
HIGHEST = lax.Precision.HIGHEST
CHUNK = 256
GROUPS = 2
LEAST = 20
EARLY = 0


def nt(left, right, precision=HIGHEST):
    return lax.dot_general(left, right, (((1,), (1,)), ((), ())), precision=precision, preferred_element_type=jnp.float32)


def nn(left, right):
    return lax.dot_general(left, right, (((1,), (0,)), ((), ())), precision=HIGHEST, preferred_element_type=jnp.float32)


def spread(column):
    return jnp.broadcast_to(column, (8, LANES))


def halves(value):
    high = value.astype(jnp.bfloat16)
    return high, (value - high.astype(jnp.float32)).astype(jnp.bfloat16)


def factor_kernel(place_ref, g_ref, pts_ref, f_ref, r_ref, pv_ref, m_ref, s_ref, l_ref, w_ref, kh_ref, kl_ref, g_last_ref, q_ref):
    dim, points = pts_ref.shape
    size = m_ref.shape[0]
    piv = size // 2
    wide = size // LANES
    scale = -1.0 / (1.65 * dim)

    for j in range(size):
        pv_ref[j : j + 1, :] = g_ref[place_ref[j // piv, j % piv]]
    pivots = jnp.concatenate([pv_ref[:piv, :dim], pv_ref[piv:, dim:]], axis=0)
    squared = pivots * pivots
    norm_row = nt(jnp.ones((8, dim), jnp.float32), squared)[0:1]
    norm_col = jnp.sum(squared, axis=1, keepdims=True)
    m_ref[...] = jnp.exp((norm_col + norm_row - 2.0 * nt(pivots, pivots)) * scale)

    sub = lax.broadcasted_iota(jnp.int32, (8, LANES), 0)
    lane = lax.broadcasted_iota(jnp.int32, (8, LANES), 1)

    def lanes(v):
        return slice(v * LANES, (v + 1) * LANES)

    trail = []
    bulk = []

    def pump(queue, count):
        for _ in range(min(count, len(queue))):
            queue.pop(0)()

    def diagonal(blk):
        start = blk * LANES
        part = [m_ref[start + 8 * g : start + 8 * g + 8, lanes(blk)] for g in range(LANES // 8)]

        def factors_of(h, off):
            return [spread(part[h][:, off + k : off + k + 1]) for k in range(8 * GROUPS)]

        def update(h, off, own, turned, factors=None):
            terms = [f * t for f, t in zip(factors or factors_of(h, off), turned)]
            while len(terms) > 1:
                terms = [p + q for p, q in zip(terms[::2], terms[1::2])]
            part[h] = jnp.where(own, 0.0, part[h]) - terms[0]

        def update_many(first, off, own, solved):
            stack = jnp.concatenate(part[first:], axis=0)
            change = nn(stack[:, off : off + 8 * GROUPS], solved)
            for n in range(len(part) - first):
                part[first + n] = jnp.where(own, 0.0, part[first + n]) - change[8 * n : 8 * n + 8]

        count = len(part)
        for g in range(0, count, GROUPS):
            base = 8 * g
            within = (lane >= base) & (lane < base + 8 * GROUPS)
            some = range(GROUPS)
            rows = [part[g + a] for a in some]
            cols = [
                [[spread(rows[a][:, base + 8 * b + k : base + 8 * b + k + 1]) for k in range(8)] for b in some]
                for a in some
            ]
            turns = []
            following = range(g + GROUPS, min(g + 2 * GROUPS, count))
            for c in some:
                off = base + 8 * c
                own = (lane >= off) & (lane < off + 8)
                eye = jnp.where(lane - off == sub, 1.0, 0.0)
                rows = [jnp.where(own, eye if a == c else 0.0, rows[a]) for a in some]
                share = -(-len(trail) // 4)
                bulk_share = -(-len(bulk) // ((count - g - c) * 4))
                if c == GROUPS - 1:
                    pump(trail, len(trail))
                    ready = {h: factors_of(h, base) for h in following}
                for j in range(8):
                    inv = spread((1.0 / cols[c][c][j])[j : j + 1])
                    scaled = [
                        (jnp.where(sub == j, 0.0, cols[a][c][j]) if a == c else cols[a][c][j]) * inv for a in some
                    ]
                    row = spread(rows[c][j : j + 1])
                    if j:
                        diag = jnp.where(sub == j, cols[c][c][j], diag)
                        turn = jnp.where(sub == j, inv, turn)
                        kept = jnp.where(sub == j, rows[c], kept)
                    else:
                        diag, turn, kept = cols[c][c][j], inv, rows[c]
                    for b in range(c, GROUPS):
                        for k in range(j + 1 if b == c else 0, 8):
                            value = spread(cols[c][b][k][j : j + 1])
                            for a in some:
                                cols[a][b][k] = cols[a][b][k] - scaled[a] * value
                    rows = [r - f * row for r, f in zip(rows, scaled)]
                    pump(trail, share)
                    if j % 2:
                        pump(bulk, bulk_share)
                turns.append(turn)
                kept = jnp.where(lane < off + 8, kept, 0.0) * lax.rsqrt(diag)
                s_ref[start + off : start + off + 8, lanes(blk)] = kept
            pump(trail, len(trail))
            solved = [r * t for r, t in zip(rows, turns)]
            turned = [spread(t[k : k + 1]) for t in solved for k in range(8)]
            for h in following:
                update(h, base, within, turned, ready[h])
            first = g + 2 * GROUPS
            stop = min(count, g + 3 * GROUPS)
            if count - stop <= LEAST:
                stop = count
            for h in range(first, stop):
                trail.append(lambda h=h, base=base, within=within, turned=turned: update(h, base, within, turned))
            if stop < count:
                together = jnp.concatenate(solved, axis=0)
                trail.append(
                    lambda stop=stop, base=base, within=within, together=together: update_many(stop, base, within, together)
                )
        pump(bulk, len(bulk))

    def block(ref, r, c):
        return ref[r * LANES : (r + 1) * LANES, lanes(c)]

    def put_upper(blk, c):
        s_ref[blk * LANES : (blk + 1) * LANES, lanes(c)] = nn(block(s_ref, blk, blk), block(m_ref, blk, c))

    def put_lower(blk, r):
        l_ref[r * LANES : (r + 1) * LANES, :] = nt(block(m_ref, r, blk), block(s_ref, blk, blk))

    def put_outer(blk, r, c):
        change = nn(l_ref[r * LANES : (r + 1) * LANES, :], block(s_ref, blk, c))
        old = 0.0 if c == blk else block(m_ref, r, c)
        m_ref[r * LANES : (r + 1) * LANES, lanes(c)] = old - change

    def put_kernel(r0):
        part = slice(r0, r0 + CHUNK)
        pts = pts_ref[:, part].T
        norm_pts = jnp.sum(pts * pts, axis=1, keepdims=True)
        kx = jnp.exp((norm_pts + norm_row - 2.0 * nt(pts, pivots)) * scale)
        g_last_ref[part, :] = kx[:, size - LANES :]
        high, low = halves(kx)
        kh_ref[part, :] = high
        kl_ref[part, :] = low

    def finish(new, part, c):
        f_ref[part, lanes(c)] = new.astype(jnp.bfloat16)
        q_ref[part, :] = new * new if c == 0 else q_ref[part, :] + new * new

    def product(left_high, left_low, weights):
        both = nt(left_high, weights, None) + nt(left_low, weights, None)
        return both[:, :LANES] + both[:, LANES:]

    def put_factor(blk, r0):
        part = slice(r0, r0 + CHUNK)
        width = (blk + 1) * LANES
        weights = w_ref[blk % 2, :, :width]
        finish(product(kh_ref[part, :width], kl_ref[part, :width], weights), part, blk)

    def put_weights(blk, value):
        high, low = halves(value)
        w_ref[blk % 2, :LANES, : value.shape[1]] = high
        w_ref[blk % 2, LANES:, : value.shape[1]] = low

    last = wide - 1

    def put_rest(r0):
        part = slice(r0, r0 + CHUNK)
        width = last * LANES
        new = product(kh_ref[part, :width], kl_ref[part, :width], w_ref[last % 2, :, :width])
        high, low = halves(g_last_ref[part, :] + new)
        kh_ref[part, lanes(last)] = high
        kl_ref[part, lanes(last)] = low

    for r0 in range(0, points, CHUNK):
        bulk.append(lambda r0=r0: put_kernel(r0))
    if EARLY:
        pump(bulk, len(bulk))
    for blk in range(wide):
        diagonal(blk)
        if blk == last:
            break
        put_upper(blk, blk + 1)
        put_lower(blk, blk + 1)
        put_outer(blk, blk + 1, blk + 1)

        def later(blk=blk):
            others = [c for c in range(wide) if c not in (blk, blk + 1)]
            for c in others:
                bulk.append(lambda c=c: put_upper(blk, c))
            for c in others + [blk]:
                bulk.append(lambda c=c: put_outer(blk, blk + 1, c))
            for r in range(blk + 2, wide):
                bulk.append(lambda r=r: put_lower(blk, r))
                for c in range(wide):
                    bulk.append(lambda r=r, c=c: put_outer(blk, r, c))
            if blk + 1 == last:
                bulk.append(lambda: put_weights(last, m_ref[last * LANES :, : last * LANES]))
                for r0 in range(0, points, CHUNK):
                    bulk.append(lambda r0=r0: put_rest(r0))
            bulk.append(lambda: put_weights(blk, s_ref[blk * LANES : (blk + 1) * LANES, : (blk + 1) * LANES]))
            for r0 in range(0, points, CHUNK):
                bulk.append(lambda r0=r0: put_factor(blk, r0))

        later()
    tail = jnp.concatenate(halves(block(s_ref, last, last)), axis=0)
    for r0 in range(0, points, CHUNK):
        part = slice(r0, r0 + CHUNK)
        finish(product(kh_ref[part, lanes(last)], kl_ref[part, lanes(last)], tail), part, last)
    r_ref[...] = 1.0 - nt(jnp.ones((8, LANES), jnp.float32), q_ref[...])[0:1]


def factor_call(place, gathered, points_t, size=512):
    dim, points = points_t.shape
    return pl.pallas_call(
        factor_kernel,
        out_shape=[
            jax.ShapeDtypeStruct((points, size), jnp.bfloat16),
            jax.ShapeDtypeStruct((1, points), jnp.float32),
        ],
        in_specs=[
            pl.BlockSpec(memory_space=pltpu.SMEM),
            pl.BlockSpec(memory_space=pltpu.VMEM),
            pl.BlockSpec(memory_space=pltpu.VMEM),
        ],
        out_specs=[pl.BlockSpec(memory_space=pltpu.VMEM)] * 2,
        scratch_shapes=[
            pltpu.VMEM((size, LANES), jnp.float32),
            pltpu.VMEM((size, size), jnp.float32),
            pltpu.VMEM((size, size), jnp.float32),
            pltpu.VMEM((size, LANES), jnp.float32),
            pltpu.VMEM((2, 2 * LANES, size), jnp.bfloat16),
            pltpu.VMEM((points, size), jnp.bfloat16),
            pltpu.VMEM((points, size), jnp.bfloat16),
            pltpu.VMEM((points, LANES), jnp.float32),
            pltpu.VMEM((points, LANES), jnp.float32),
        ],
        compiler_params=pltpu.CompilerParams(vmem_limit_bytes=40 << 20),
        name="factor",
    )(place, gathered, points_t)


def body(points_t, pivots):
    gathered, place = exchange(points_t, pivots)
    factor, resid = factor_call(place, gathered, points_t)
    return (factor, resid.reshape(-1))


def solution(mesh):
    return jax.shard_map(
        body,
        mesh=mesh,
        in_specs=(P(None, "rows"), P()),
        out_specs=(P("rows", None), P("rows")),
        check_vma=False,
    )
```

```python
import jax
import jax.numpy as jnp
from jax import lax
from jax.experimental import pallas as pl
from jax.experimental.pallas import tpu as pltpu
from jax.sharding import PartitionSpec as P

NX, NZ, NY, NC = 4, 8, 4, 2
CAP = 3
NEAR = 5
HALF = NX * NY * NZ * CAP
FAR_AT = NX * NY * NEAR * CAP
BIG = 1 << 24
MESH = pl.DeviceIdType.MESH


def exchange_kernel(piv_ref, pts_hbm, out_ref, place_ref, pts_ref, pts_sem, zs, zr, ps, pr, cs, cr):
    me = lax.axis_index("rows")
    core = lax.rem(me, NC)
    y = lax.rem(me // NC, NY)
    z = lax.rem(me // (NC * NY), NZ)
    x = me // (NC * NY * NZ)

    def device(x_, y_, z_, core_):
        return ((x_ * NZ + z_) * NY + y_) * NC + core_

    def z_peer(k):
        return device(x, y, lax.rem(z + k, NZ), core)

    flat = [(2, 2), (2, 1), (1, 2), (2, 3), (3, 2), (1, 1), (3, 3), (1, 3), (3, 1)]
    flat += [(0, 2), (2, 0), (0, 1), (1, 0), (0, 3), (3, 0)]

    def plane_peer(i, k):
        return device(lax.rem(x + i, NX), lax.rem(y + k, NY), z, core)

    sibling = device(x, y, z, 1 - core)
    peers = [z_peer(k) for k in range(1, NZ)] + [plane_peer(i, k) for i, k in flat] + [sibling]
    barrier = pltpu.get_barrier_semaphore()
    for peer in peers:
        pl.semaphore_signal(barrier, inc=1, device_id=(peer,), device_id_type=MESH)
    load = pltpu.make_async_copy(pts_hbm, pts_ref, pts_sem)
    load.start()

    rows_here = pts_ref.shape[1]
    pivots = piv_ref[...]
    local = pivots - me * rows_here
    key = jnp.where((local >= 0) & (local < rows_here), local, BIG)
    floor = jnp.full((2, 1), -1, jnp.int32)
    lanes = lax.broadcasted_iota(jnp.int32, (2, rows_here), 1)
    picks = []
    for _ in range(CAP):
        floor = jnp.min(jnp.where(key > floor, key, BIG), axis=1, keepdims=True)
        picks.append(jnp.where(lanes == floor, 1.0, 0.0).astype(jnp.float32))
    pad = jnp.zeros((1, rows_here), jnp.float32)
    pick = jnp.concatenate([p[0:1] for p in picks] + [pad] + [p[1:2] for p in picks] + [pad], axis=0)
    load.wait()
    slots = lax.dot_general(
        pick,
        pts_ref[...],
        (((1,), (1,)), ((), ())),
        precision=lax.Precision.HIGHEST,
        preferred_element_type=jnp.float32,
    )
    both = jnp.concatenate([slots[0:4], slots[4:8]], axis=1)

    def near_at(core_, plane):
        return core_ * HALF + plane * (NEAR * CAP)

    def far_at(core_, plane):
        return core_ * HALF + FAR_AT + plane * ((NZ - NEAR) * CAP)

    def chunk_at(core_, plane, step):
        zz = (step + 2) % NZ
        if zz < NEAR:
            return near_at(core_, plane) + zz * CAP
        return far_at(core_, plane) + (zz - NEAR) * CAP

    here = x * NY + y
    mine = chunk_at(core, here, 0)
    for s in range(CAP):
        out_ref[mine + s] = both[s : s + 1]
    pl.semaphore_wait(barrier, len(peers))

    def remote(src, dst, count, send_sem, recv_sem, peer):
        return pltpu.make_async_remote_copy(
            src_ref=out_ref.at[pl.ds(src, count)],
            dst_ref=out_ref.at[pl.ds(dst, count)],
            send_sem=send_sem,
            recv_sem=recv_sem,
            device_id=(peer,),
            device_id_type=MESH,
        )

    sent = []

    def send(*what):
        copy = remote(*what)
        copy.start()
        sent.append(copy)

    near_steps = [1, NZ - 1, 2, NZ - 2]
    far_steps = [k for k in range(1, NZ) if k not in near_steps]
    for k in far_steps + near_steps:
        send(mine, chunk_at(core, here, -k), CAP, zs.at[k - 1], zr.at[k - 1], z_peer(k))

    as_float = jnp.concatenate([pivots, jnp.zeros((6, pivots.shape[1]), jnp.int32)], axis=0).astype(jnp.float32)
    columns = jnp.transpose(as_float)
    ranks = []
    for block in range(2):
        other = columns[:, block : block + 1]
        row = as_float[block : block + 1]
        first = ((pivots[block : block + 1] // rows_here) * rows_here).astype(jnp.float32)
        before = (other < row) & (other >= first)
        ranks.append(jnp.sum(jnp.where(before, 1.0, 0.0), axis=0, keepdims=True))
    rank = jnp.concatenate(ranks, axis=0).astype(jnp.int32)
    owner = pivots // rows_here
    o_core = lax.rem(owner, NC)
    o_y = lax.rem(owner // NC, NY)
    o_z = lax.rem(owner // (NC * NY), NZ)
    o_x = owner // (NC * NY * NZ)
    o_plane = o_x * NY + o_y
    zz = lax.rem(o_z - z + (NZ + 2), NZ)
    place_ref[...] = (
        jnp.where(
            zz < NEAR,
            near_at(o_core, o_plane) + zz * CAP,
            far_at(o_core, o_plane) + (zz - NEAR) * CAP,
        )
        + rank
    )

    def z_arrived(k):
        remote(mine, chunk_at(core, here, -k), CAP, zs.at[k - 1], zr.at[k - 1], z_peer(k)).wait_recv()

    for group, steps, at, count in (
        (0, near_steps, near_at, NEAR * CAP),
        (1, far_steps, far_at, (NZ - NEAR) * CAP),
    ):
        for k in steps:
            z_arrived(k)
        for n, (i, k) in enumerate(flat):
            send(at(core, here), at(core, here), count, ps.at[group, n], pr.at[group, n], plane_peer(i, k))
    for group, at, count in ((0, near_at, NEAR * CAP), (1, far_at, (NZ - NEAR) * CAP)):
        for n, (i, k) in enumerate(flat):
            source = lax.rem(x + NX - i, NX) * NY + lax.rem(y + NY - k, NY)
            remote(at(core, source), at(core, source), count, ps.at[group, n], pr.at[group, n], plane_peer(i, k)).wait_recv()
        send(at(core, 0), at(core, 0), count * NX * NY, cs.at[group], cr.at[group], sibling)
    for group, at, count in ((0, near_at, NEAR * CAP), (1, far_at, (NZ - NEAR) * CAP)):
        remote(
            at(1 - core, 0), at(1 - core, 0), count * NX * NY, cs.at[group], cr.at[group], sibling
        ).wait_recv()
    for copy in sent:
        copy.wait_send()


def exchange(points_t, pivots):
    return pl.pallas_call(
        exchange_kernel,
        out_shape=[
            pltpu.VMEM((NC * HALF, 1, 128), jnp.float32),
            pltpu.VMEM(pivots.shape, jnp.int32),
        ],
        in_specs=[pl.BlockSpec(memory_space=pltpu.VMEM), pl.BlockSpec(memory_space=pl.ANY)],
        out_specs=[pl.BlockSpec(memory_space=pltpu.VMEM)] * 2,
        scratch_shapes=[
            pltpu.VMEM(points_t.shape, jnp.float32),
            pltpu.SemaphoreType.DMA(()),
            pltpu.SemaphoreType.DMA((NZ - 1,)),
            pltpu.SemaphoreType.DMA((NZ - 1,)),
            pltpu.SemaphoreType.DMA((2, NX * NY - 1)),
            pltpu.SemaphoreType.DMA((2, NX * NY - 1)),
            pltpu.SemaphoreType.DMA((2,)),
            pltpu.SemaphoreType.DMA((2,)),
        ],
        compiler_params=pltpu.CompilerParams(collective_id=0, has_side_effects=True),
        name="exchange",
    )(pivots, points_t)


LANES = 128
HIGHEST = lax.Precision.HIGHEST
CHUNK = 256
GROUPS = 2
LEAST = 20
EARLY = 0


def nt(left, right, precision=HIGHEST):
    return lax.dot_general(left, right, (((1,), (1,)), ((), ())), precision=precision, preferred_element_type=jnp.float32)


def nn(left, right):
    return lax.dot_general(left, right, (((1,), (0,)), ((), ())), precision=HIGHEST, preferred_element_type=jnp.float32)


def spread(column):
    return jnp.broadcast_to(column, (8, LANES))


def halves(value):
    high = value.astype(jnp.bfloat16)
    return high, (value - high.astype(jnp.float32)).astype(jnp.bfloat16)


def factor_kernel(place_ref, g_ref, pts_ref, f_ref, r_ref, pv_ref, m_ref, s_ref, l_ref, w_ref, kh_ref, kl_ref, g_last_ref, q_ref):
    dim, points = pts_ref.shape
    size = m_ref.shape[0]
    piv = size // 2
    wide = size // LANES
    scale = -1.0 / (1.65 * dim)

    for j in range(size):
        pv_ref[j : j + 1, :] = g_ref[place_ref[j // piv, j % piv]]
    pivots = jnp.concatenate([pv_ref[:piv, :dim], pv_ref[piv:, dim:]], axis=0)
    squared = pivots * pivots
    norm_row = nt(jnp.ones((8, dim), jnp.float32), squared)[0:1]
    norm_col = jnp.sum(squared, axis=1, keepdims=True)
    m_ref[...] = jnp.exp((norm_col + norm_row - 2.0 * nt(pivots, pivots)) * scale)

    sub = lax.broadcasted_iota(jnp.int32, (8, LANES), 0)
    lane = lax.broadcasted_iota(jnp.int32, (8, LANES), 1)

    def lanes(v):
        return slice(v * LANES, (v + 1) * LANES)

    trail = []
    bulk = []

    def pump(queue, count):
        for _ in range(min(count, len(queue))):
            queue.pop(0)()

    def diagonal(blk):
        start = blk * LANES
        part = [m_ref[start + 8 * g : start + 8 * g + 8, lanes(blk)] for g in range(LANES // 8)]

        def factors_of(h, off):
            return [spread(part[h][:, off + k : off + k + 1]) for k in range(8 * GROUPS)]

        def update(h, off, own, turned, factors=None):
            terms = [f * t for f, t in zip(factors or factors_of(h, off), turned)]
            while len(terms) > 1:
                terms = [p + q for p, q in zip(terms[::2], terms[1::2])]
            part[h] = jnp.where(own, 0.0, part[h]) - terms[0]

        def update_many(first, off, own, solved):
            stack = jnp.concatenate(part[first:], axis=0)
            change = nn(stack[:, off : off + 8 * GROUPS], solved)
            for n in range(len(part) - first):
                part[first + n] = jnp.where(own, 0.0, part[first + n]) - change[8 * n : 8 * n + 8]

        count = len(part)
        for g in range(0, count, GROUPS):
            base = 8 * g
            within = (lane >= base) & (lane < base + 8 * GROUPS)
            some = range(GROUPS)
            rows = [part[g + a] for a in some]
            cols = [
                [[spread(rows[a][:, base + 8 * b + k : base + 8 * b + k + 1]) for k in range(8)] for b in some]
                for a in some
            ]
            turns = []
            following = range(g + GROUPS, min(g + 2 * GROUPS, count))
            for c in some:
                off = base + 8 * c
                own = (lane >= off) & (lane < off + 8)
                eye = jnp.where(lane - off == sub, 1.0, 0.0)
                rows = [jnp.where(own, eye if a == c else 0.0, rows[a]) for a in some]
                share = -(-len(trail) // 4)
                bulk_share = -(-len(bulk) // ((count - g - c) * 4))
                if c == GROUPS - 1:
                    pump(trail, len(trail))
                    ready = {h: factors_of(h, base) for h in following}
                for j in range(8):
                    inv = spread((1.0 / cols[c][c][j])[j : j + 1])
                    scaled = [
                        (jnp.where(sub == j, 0.0, cols[a][c][j]) if a == c else cols[a][c][j]) * inv for a in some
                    ]
                    row = spread(rows[c][j : j + 1])
                    if j:
                        diag = jnp.where(sub == j, cols[c][c][j], diag)
                        turn = jnp.where(sub == j, inv, turn)
                        kept = jnp.where(sub == j, rows[c], kept)
                    else:
                        diag, turn, kept = cols[c][c][j], inv, rows[c]
                    for b in range(c, GROUPS):
                        for k in range(j + 1 if b == c else 0, 8):
                            value = spread(cols[c][b][k][j : j + 1])
                            for a in some:
                                cols[a][b][k] = cols[a][b][k] - scaled[a] * value
                    rows = [r - f * row for r, f in zip(rows, scaled)]
                    pump(trail, share)
                    if j % 2:
                        pump(bulk, bulk_share)
                turns.append(turn)
                kept = jnp.where(lane < off + 8, kept, 0.0) * lax.rsqrt(diag)
                s_ref[start + off : start + off + 8, lanes(blk)] = kept
            pump(trail, len(trail))
            solved = [r * t for r, t in zip(rows, turns)]
            turned = [spread(t[k : k + 1]) for t in solved for k in range(8)]
            for h in following:
                update(h, base, within, turned, ready[h])
            first = g + 2 * GROUPS
            stop = min(count, g + 3 * GROUPS)
            if count - stop <= LEAST:
                stop = count
            for h in range(first, stop):
                trail.append(lambda h=h, base=base, within=within, turned=turned: update(h, base, within, turned))
            if stop < count:
                together = jnp.concatenate(solved, axis=0)
                trail.append(
                    lambda stop=stop, base=base, within=within, together=together: update_many(stop, base, within, together)
                )
        pump(bulk, len(bulk))

    def block(ref, r, c):
        return ref[r * LANES : (r + 1) * LANES, lanes(c)]

    def put_upper(blk, c):
        s_ref[blk * LANES : (blk + 1) * LANES, lanes(c)] = nn(block(s_ref, blk, blk), block(m_ref, blk, c))

    def put_lower(blk, r):
        l_ref[r * LANES : (r + 1) * LANES, :] = nt(block(m_ref, r, blk), block(s_ref, blk, blk))

    def put_outer(blk, r, c):
        change = nn(l_ref[r * LANES : (r + 1) * LANES, :], block(s_ref, blk, c))
        old = 0.0 if c == blk else block(m_ref, r, c)
        m_ref[r * LANES : (r + 1) * LANES, lanes(c)] = old - change

    def put_kernel(r0):
        part = slice(r0, r0 + CHUNK)
        pts = pts_ref[:, part].T
        norm_pts = jnp.sum(pts * pts, axis=1, keepdims=True)
        kx = jnp.exp((norm_pts + norm_row - 2.0 * nt(pts, pivots)) * scale)
        g_last_ref[part, :] = kx[:, size - LANES :]
        high, low = halves(kx)
        kh_ref[part, :] = high
        kl_ref[part, :] = low

    def finish(new, part, c):
        f_ref[part, lanes(c)] = new.astype(jnp.bfloat16)
        q_ref[part, :] = new * new if c == 0 else q_ref[part, :] + new * new

    def product(left_high, left_low, weights):
        both = nt(left_high, weights, None) + nt(left_low, weights, None)
        return both[:, :LANES] + both[:, LANES:]

    def put_factor(blk, r0):
        part = slice(r0, r0 + CHUNK)
        width = (blk + 1) * LANES
        weights = w_ref[blk % 2, :, :width]
        finish(product(kh_ref[part, :width], kl_ref[part, :width], weights), part, blk)

    def put_weights(blk, value):
        high, low = halves(value)
        w_ref[blk % 2, :LANES, : value.shape[1]] = high
        w_ref[blk % 2, LANES:, : value.shape[1]] = low

    last = wide - 1

    def put_rest(r0):
        part = slice(r0, r0 + CHUNK)
        width = last * LANES
        new = product(kh_ref[part, :width], kl_ref[part, :width], w_ref[last % 2, :, :width])
        high, low = halves(g_last_ref[part, :] + new)
        kh_ref[part, lanes(last)] = high
        kl_ref[part, lanes(last)] = low

    for r0 in range(0, points, CHUNK):
        bulk.append(lambda r0=r0: put_kernel(r0))
    if EARLY:
        pump(bulk, len(bulk))
    for blk in range(wide):
        diagonal(blk)
        if blk == last:
            break
        put_upper(blk, blk + 1)
        put_lower(blk, blk + 1)
        put_outer(blk, blk + 1, blk + 1)

        def later(blk=blk):
            others = [c for c in range(wide) if c not in (blk, blk + 1)]
            for c in others:
                bulk.append(lambda c=c: put_upper(blk, c))
            for c in others + [blk]:
                bulk.append(lambda c=c: put_outer(blk, blk + 1, c))
            for r in range(blk + 2, wide):
                bulk.append(lambda r=r: put_lower(blk, r))
                for c in range(wide):
                    bulk.append(lambda r=r, c=c: put_outer(blk, r, c))
            if blk + 1 == last:
                bulk.append(lambda: put_weights(last, m_ref[last * LANES :, : last * LANES]))
                for r0 in range(0, points, CHUNK):
                    bulk.append(lambda r0=r0: put_rest(r0))
            bulk.append(lambda: put_weights(blk, s_ref[blk * LANES : (blk + 1) * LANES, : (blk + 1) * LANES]))
            for r0 in range(0, points, CHUNK):
                bulk.append(lambda r0=r0: put_factor(blk, r0))

        later()
    tail = jnp.concatenate(halves(block(s_ref, last, last)), axis=0)
    for r0 in range(0, points, CHUNK):
        part = slice(r0, r0 + CHUNK)
        finish(product(kh_ref[part, lanes(last)], kl_ref[part, lanes(last)], tail), part, last)
    r_ref[...] = 1.0 - nt(jnp.ones((8, LANES), jnp.float32), q_ref[...])[0:1]


def factor_call(place, gathered, points_t, size=512):
    dim, points = points_t.shape
    return pl.pallas_call(
        factor_kernel,
        out_shape=[
            jax.ShapeDtypeStruct((points, size), jnp.bfloat16),
            jax.ShapeDtypeStruct((1, points), jnp.float32),
        ],
        in_specs=[
            pl.BlockSpec(memory_space=pltpu.SMEM),
            pl.BlockSpec(memory_space=pltpu.VMEM),
            pl.BlockSpec(memory_space=pltpu.VMEM),
        ],
        out_specs=[pl.BlockSpec(memory_space=pltpu.VMEM)] * 2,
        scratch_shapes=[
            pltpu.VMEM((size, LANES), jnp.float32),
            pltpu.VMEM((size, size), jnp.float32),
            pltpu.VMEM((size, size), jnp.float32),
            pltpu.VMEM((size, LANES), jnp.float32),
            pltpu.VMEM((2, 2 * LANES, size), jnp.bfloat16),
            pltpu.VMEM((points, size), jnp.bfloat16),
            pltpu.VMEM((points, size), jnp.bfloat16),
            pltpu.VMEM((points, LANES), jnp.float32),
            pltpu.VMEM((points, LANES), jnp.float32),
        ],
        compiler_params=pltpu.CompilerParams(vmem_limit_bytes=40 << 20),
        name="factor",
    )(place, gathered, points_t)


def body(points_t, pivots):
    gathered, place = exchange(points_t, pivots)
    factor, resid = factor_call(place, gathered, points_t)
    return (factor, resid.reshape(-1))


def solution(mesh):
    return jax.shard_map(
        body,
        mesh=mesh,
        in_specs=(P(None, "rows"), P()),
        out_specs=(P("rows", None), P("rows")),
        check_vma=False,
    )
```
